32 devices in a mesh: energy: 8 (over z, y), slab: 4 (over x, core).
Axes of the slice: x: 2, y: 2, z: 4, core: 2. Of those that a mesh axis runs over, the one named last changes fastest.
Arguments:
- green: bfloat16 [8, 4, 2, 512, 512], P('energy', 'slab'), may hold values from -3 to 3
- sigma: bfloat16 [8, 4, 2, 512, 512], P('energy', 'slab'), may hold values from -0.035888672 to 0.035888672
- tiles: int32 [4, 16], P('slab'), may hold values from 0 to 511, as said below
- owner: int32 [4, 16], P('slab'), may hold values from 0 to 7, as said below
- energy_order: int32 [8], replicated, may hold values from 0 to 7, each once
Outputs:
- polar: bfloat16 [4, 32, 2, 8, 1, 512], P('slab', 'energy')
The draws below stay inside these ranges and needn't reach their ends.
Inputs may be any that keep to these rules, and one draw needn't show every extreme that they name: The tiles of one slab are distinct. No owner holds more than 4 tiles of one slab; in every slab some owner holds exactly 4.
All inputs are finite; a program needn't handle non-finite values.
Results may differ from the reference program's by a relative error of at most 0.008.
Values may be sent and summed in bfloat16 or wider, within the bound.
A program may use at most 64 MiB of HBM per device.

```python
import jax
import jax.numpy as jnp
from jax import lax

BLOCK = 512
STRIP = 1
CAP = 4
LISTED = 16
NTILES = 512
NE = 8
NFFT = 16
NS = 4
SLOTS = 32
N_ENERGY = 8


def draw_tiles(key, part):
    keys = jax.random.split(jax.random.fold_in(key, 11), NS)

    def one(k):
        return jax.random.permutation(k, NTILES)[:LISTED].astype(jnp.int32)
    return jax.vmap(one)(keys)


def draw_owner(key, part):
    keys = jax.random.split(jax.random.fold_in(key, 23), NS)

    def one(k):
        k_one, k_two, k_three = jax.random.split(k, 3)
        order_keys = jax.random.permutation(k_one, SLOTS).astype(jnp.int32)
        leader = jax.random.randint(k_two, (), 0, N_ENERGY).astype(jnp.int32)
        slot_ids = jnp.arange(SLOTS, dtype=jnp.int32)
        order_keys = jnp.where(slot_ids // CAP == leader, -1 - slot_ids, order_keys)
        chosen = jnp.argsort(order_keys)[:LISTED].astype(jnp.int32)
        chosen = chosen[jax.random.permutation(k_three, LISTED)]
        return (chosen // CAP).astype(jnp.int32)
    return jax.vmap(one)(keys)


def block_levels(key, dims, shards, low, largest):
    factor_of, own = 1.0, jax.random.fold_in(key, 6)
    for dim, blocks in shards:
        heights = jnp.exp(jax.random.uniform(jax.random.fold_in(own, dim), (blocks,), jnp.float32, low / len(shards), largest / len(shards)))
        factor_of = factor_of * jnp.repeat(heights, dims[dim] // blocks).reshape([-1 if axis == dim else 1 for axis in range(len(dims))])
    return factor_of


def noise(key, extent, scale, limit, shards=(), kind=jnp.bfloat16):
    result = jax.random.normal(key, extent, jnp.float32) * scale
    if len(shards) > 0:
        result = block_levels(key, extent, shards, -0.22, 0.18) * result
    return jnp.clip(result, min=-limit, max=limit).astype(kind)


def setup_inputs(seed: int = 0) -> dict:
    key_of = jax.random.split(jax.random.key(seed), 6)
    green = noise(key_of[0], (NE, NS, 2, BLOCK, BLOCK), 0.5, 3.0, ((0, 8), (1, 4)))
    sigma = noise(key_of[1], (NE, NS, 2, BLOCK, BLOCK), 0.006, 0.035888672, ((0, 8), (1, 4)))
    tiles = draw_tiles(jax.random.fold_in(key_of[5], 71), 0)
    owner = draw_owner(jax.random.fold_in(key_of[5], 71), 0)
    energy_order = jax.random.permutation(key_of[4], NE).astype(jnp.int32)
    return dict(green=green, sigma=sigma, tiles=tiles, owner=owner, energy_order=energy_order)


def ranks_of(own):
    pos = jnp.arange(own.shape[0], dtype=jnp.int32)
    same = (own[:, None] == own[None, :]) & (pos[:, None] < pos[None, :])
    return jnp.sum(same.astype(jnp.int32), axis=0).astype(jnp.int32)


def one_block(green_block, beside_all, rows):
    eff = (beside_all[0].astype(jnp.float32) + beside_all[1].astype(jnp.float32) + beside_all[2].astype(jnp.float32)).astype(jnp.bfloat16)
    g_re, g_im = green_block[0], green_block[1]
    s_re, s_im = eff[0], eff[1]
    p_re = (jnp.dot(g_re, s_re, preferred_element_type=jnp.float32) - jnp.dot(g_im, s_im, preferred_element_type=jnp.float32)).astype(jnp.bfloat16)
    p_im = (jnp.dot(g_re, s_im, preferred_element_type=jnp.float32) + jnp.dot(g_im, s_re, preferred_element_type=jnp.float32)).astype(jnp.bfloat16)
    a_re = p_re[rows]
    a_im = p_im[rows]
    l_re = jnp.dot(a_re, g_re.T, preferred_element_type=jnp.float32) + jnp.dot(a_im, g_im.T, preferred_element_type=jnp.float32)
    l_im = jnp.dot(a_im, g_re.T, preferred_element_type=jnp.float32) - jnp.dot(a_re, g_im.T, preferred_element_type=jnp.float32)
    d_re = g_re[rows].astype(jnp.float32) - g_re[:, rows].T.astype(jnp.float32)
    d_im = g_im[rows].astype(jnp.float32) + g_im[:, rows].T.astype(jnp.float32)
    return jnp.stack([l_re.astype(jnp.bfloat16), l_im.astype(jnp.bfloat16), (l_re + d_re).astype(jnp.bfloat16), (l_im + d_im).astype(jnp.bfloat16)])


def reference(green, sigma, tiles, owner, energy_order):
    row_table = (tiles[:, :, None] * STRIP + jnp.arange(STRIP, dtype=jnp.int32)[None, None, :]).reshape(NS, LISTED * STRIP).astype(jnp.int32)

    def per_energy(pair):
        green_e, sigma_e = pair
        padded = jnp.concatenate([jnp.zeros_like(sigma_e[:1]), sigma_e, jnp.zeros_like(sigma_e[:1])], axis=0)

        def per_slab(idx):
            beside_all = lax.dynamic_slice_in_dim(padded, idx, 3, 0)
            return one_block(green_e[idx], beside_all, row_table[idx])

        return lax.map(per_slab, jnp.arange(NS, dtype=jnp.int32))

    planes = lax.map(per_energy, (green, sigma))
    inverse = jnp.argsort(energy_order).astype(jnp.int32)
    planes = planes[inverse]

    def per_slab_out(idx):
        data = planes[:, idx].astype(jnp.float32)
        lesser = lax.complex(data[:, 0], data[:, 1])
        greater = lax.complex(data[:, 2], data[:, 3])
        spec_l = jnp.fft.fft(lesser, n=NFFT, axis=0)
        spec_g = jnp.fft.fft(greater, n=NFFT, axis=0)
        corr = jnp.fft.ifft(spec_l * jnp.conj(spec_g), axis=0)[:NE] / NE
        vals = jnp.stack([jnp.real(corr), jnp.imag(corr)], axis=1)
        vals = vals.reshape(NE, 2, LISTED, STRIP, BLOCK).transpose(2, 1, 0, 3, 4)
        own = owner[idx]
        slot = (own * CAP + ranks_of(own)).astype(jnp.int32)
        base = jnp.zeros((SLOTS, 2, NE, STRIP, BLOCK), vals.dtype)
        return base.at[slot].set(vals).astype(jnp.bfloat16)

    return lax.map(per_slab_out, jnp.arange(NS, dtype=jnp.int32))
```

```python
import functools

import jax
import jax.numpy as jnp
from jax import lax
from jax.experimental import pallas as pl
from jax.experimental.pallas import tpu as pltpu
from jax.sharding import PartitionSpec as P

CAP = 4
LANES = 128
MESH = pl.DeviceIdType.MESH
F32 = jnp.float32
BF16 = jnp.bfloat16


def iota(shape, dim):
    return lax.broadcasted_iota(jnp.int32, shape, dim)


def repeat(first, last, body):
    if last - first <= 16:
        for k in range(first, last):
            body(k)
    else:
        @pl.loop(first, last)
        def _(k):
            body(k)


def column_of(row, length):
    spread = jnp.broadcast_to(row, (length, length))
    eye = iota((length, length), 0) == iota((length, length), 1)
    return jnp.sum(jnp.where(eye, spread, 0.0), axis=1, keepdims=True)


def dot(left, right):
    return jnp.dot(left, right, preferred_element_type=F32)


def dot_t(left, right):
    return lax.dot_general(left, right, (((1,), (1,)), ((), ())), preferred_element_type=F32)


def kernel(
    count,
    slabs,
    green,
    sigma,
    tiles,
    owner,
    order,
    out,
    g_v,
    s_v,
    tiles_v,
    owner_v,
    order_v,
    inverse,
    a_own,
    a_in,
    q_out,
    q_in,
    p_sum,
    d_out,
    d_in,
    l_out,
    l_in,
    lags,
    load_sem,
    slab_send,
    slab_recv,
    d_send,
    d_recv,
    l_send,
    l_recv,
):
    block = g_v.shape[-1]
    listed = tiles_v.shape[-1]
    rows = 2 * CAP
    me = lax.axis_index("energy")
    slab = lax.axis_index("slab")
    parity = lax.rem(slab, 2)
    near = slab + 1 - 2 * parity
    far = slab - 1 + 2 * parity
    has_far = jnp.logical_and(far >= 0, far < slabs)

    loads = [
        pltpu.make_async_copy(tiles, tiles_v, load_sem.at[0]),
        pltpu.make_async_copy(owner, owner_v, load_sem.at[1]),
        pltpu.make_async_copy(order, order_v, load_sem.at[2]),
        pltpu.make_async_copy(green.at[0, 0], g_v, load_sem.at[3]),
        pltpu.make_async_copy(sigma.at[0, 0], s_v, load_sem.at[4]),
    ]
    for load in loads:
        load.start()

    barrier = pltpu.get_barrier_semaphore()

    def greet(k):
        pl.semaphore_signal(
            barrier, inc=1, device_id={"energy": lax.rem(me + k, count)}, device_id_type=MESH
        )

    repeat(1, count, greet)
    pl.semaphore_signal(barrier, inc=1, device_id={"slab": near}, device_id_type=MESH)

    @pl.when(has_far)
    def _():
        pl.semaphore_signal(barrier, inc=1, device_id={"slab": far}, device_id_type=MESH)

    loads[0].wait()
    tile_col = column_of(tiles_v[...].astype(F32), listed)
    onehot = (iota((listed, block), 1).astype(F32) == tile_col).astype(BF16)
    loads[1].wait()
    own_row = owner_v[...].astype(F32)
    own_col = column_of(own_row, listed)
    earlier = (own_col == own_row) & (iota((listed, listed), 1) < iota((listed, listed), 0))
    rank_col = jnp.sum(jnp.where(earlier, 1.0, 0.0), axis=1, keepdims=True)
    slot_col = own_col * CAP + rank_col
    wide = (listed, 2 * listed)
    spread = iota(wide, 0) == lax.rem(iota(wide, 1), listed)
    slot_row = jnp.sum(jnp.where(spread, slot_col, 0.0), axis=0, keepdims=True)
    full = (count * rows, 2 * listed)
    line = iota(full, 0)
    plane = lax.rem(line, rows) // CAP
    slot = (line // rows) * CAP + lax.rem(line, CAP)
    selector = (
        (slot.astype(F32) == slot_row) & (plane == iota(full, 1) // listed)
    ).astype(BF16)

    loads[3].wait()
    row_re = dot(onehot, g_v[0])
    row_im = dot(onehot, g_v[1])
    a_own[0:listed, :] = row_re.astype(BF16)
    a_own[listed : 2 * listed, :] = row_im.astype(BF16)
    d_re = row_re - dot_t(onehot, g_v[0])
    d_im = row_im + dot_t(onehot, g_v[1])
    d_all = jnp.concatenate([d_re, d_im], axis=0).astype(BF16)
    d_out[...] = dot(selector, d_all).astype(BF16).reshape(count, rows, block)

    pl.semaphore_wait(barrier, count + has_far.astype(jnp.int32))

    def to_slab(src, dst, k, target):
        return pltpu.make_async_remote_copy(
            src_ref=src,
            dst_ref=dst,
            send_sem=slab_send.at[k],
            recv_sem=slab_recv.at[k],
            device_id={"slab": target},
            device_id_type=MESH,
        )

    a_far = to_slab(a_own, a_in.at[1], 1, far)
    a_near = to_slab(a_own, a_in.at[0], 0, near)
    q_far = to_slab(q_out.at[1], q_in.at[1], 3, far)
    q_near = to_slab(q_out.at[0], q_in.at[0], 2, near)

    def to_peer(src, dst, send, recv, k):
        peer = lax.rem(me + k, count)
        return pltpu.make_async_remote_copy(
            src_ref=src.at[peer],
            dst_ref=dst.at[me],
            send_sem=send.at[k],
            recv_sem=recv.at[k],
            device_id={"energy": peer},
            device_id_type=MESH,
        )

    @pl.when(has_far)
    def _():
        a_far.start()

    a_near.start()
    repeat(1, count, lambda k: to_peer(d_out, d_in, d_send, d_recv, k).start())
    d_in[me] = d_out[me]

    loads[2].wait()

    def invert(target):
        def step(k, total):
            return jnp.where(order_v[k] == target, k, total)

        inverse[target] = lax.fori_loop(0, count, step, jnp.int32(0), unroll=count <= 16)

    repeat(0, count, invert)

    def times_sigma(a):
        with_re = dot(a, s_v[0])
        with_im = dot(a, s_v[1])
        return (
            with_re[:listed] - with_im[listed:],
            with_im[:listed] + with_re[listed:],
        )

    loads[4].wait()
    own_re, own_im = times_sigma(a_own[...])
    p_sum[0:listed, :] = own_re
    p_sum[listed : 2 * listed, :] = own_im

    def answer(k):
        part_re, part_im = times_sigma(a_in[k])
        q_out[k, 0:listed, :] = part_re.astype(BF16)
        q_out[k, listed : 2 * listed, :] = part_im.astype(BF16)

    a_near.wait_recv()
    answer(0)
    q_near.start()

    @pl.when(has_far)
    def _():
        a_far.wait_recv()
        answer(1)
        q_far.start()

    q_near.wait_recv()
    p_sum[...] += q_in[0].astype(F32)

    @pl.when(has_far)
    def _():
        q_far.wait_recv()
        p_sum[...] += q_in[1].astype(F32)

    p_all = p_sum[...].astype(BF16)
    with_re = dot_t(p_all, g_v[0])
    with_im = dot_t(p_all, g_v[1])
    l_re = with_re[:listed] + with_im[listed:]
    l_im = with_re[listed:] - with_im[:listed]
    l_all = jnp.concatenate([l_re, l_im], axis=0).astype(BF16)
    l_out[...] = dot(selector, l_all).astype(BF16).reshape(count, rows, block)
    repeat(1, count, lambda k: to_peer(l_out, l_in, l_send, l_recv, k).start())
    l_in[me] = l_out[me]

    def arrived(k):
        to_peer(d_out, d_in, d_send, d_recv, k).wait()
        to_peer(l_out, l_in, l_send, l_recv, k).wait()

    repeat(1, count, arrived)

    def lesser_at(point):
        return l_in[inverse[point]].astype(F32)

    def greater_at(point):
        source = inverse[point]
        return l_in[source].astype(F32) + d_in[source].astype(F32)

    upper = iota((rows, block), 0) < CAP

    def finish(straight, crossed):
        return jnp.where(
            upper,
            straight + pltpu.roll(straight, CAP, 0),
            crossed - pltpu.roll(crossed, CAP, 0),
        ) * (1.0 / count)

    def keep(value, where):
        for chunk in range(block // LANES):
            lags[chunk, where, :] = value[:, chunk * LANES : (chunk + 1) * LANES]

    if count <= 8:
        lesser = [lesser_at(e) for e in range(count)]
        greater = [greater_at(e) for e in range(count)]
        swapped = [pltpu.roll(value, CAP, 0) for value in greater]
        for lag in range(count):
            pairs = range(count - lag)
            straight = sum(lesser[e + lag] * greater[e] for e in pairs)
            crossed = sum(lesser[e + lag] * swapped[e] for e in pairs)
            keep(finish(straight, crossed), pl.ds(lag * rows, rows))
    else:
        @pl.loop(0, count)
        def _(lag):
            def step(e, sums):
                left = lesser_at(e + lag)
                right = greater_at(e)
                return (sums[0] + left * right, sums[1] + left * pltpu.roll(right, CAP, 0))

            zero = jnp.zeros((rows, block), F32)
            straight, crossed = lax.fori_loop(0, count - lag, step, (zero, zero))
            keep(finish(straight, crossed), pl.ds(pl.multiple_of(lag * rows, rows), rows))

    for part in range(2):
        for slot_index in range(CAP):
            for chunk in range(block // LANES):
                out[slot_index, part, :, chunk * LANES : (chunk + 1) * LANES] = lags[
                    chunk, pl.ds(part * CAP + slot_index, count, stride=rows), :
                ].astype(BF16)

    a_near.wait_send()
    q_near.wait_send()

    @pl.when(has_far)
    def _():
        a_far.wait_send()
        q_far.wait_send()


def on_device(green, sigma, tiles, owner, energy_order):
    block = green.shape[-1]
    listed = tiles.shape[1]
    count = lax.axis_size("energy")
    slabs = lax.axis_size("slab")
    rows = 2 * CAP
    anywhere = pl.BlockSpec(memory_space=pl.ANY)
    result = pl.pallas_call(
        functools.partial(kernel, count, slabs),
        out_shape=jax.ShapeDtypeStruct((CAP, 2, count, block), BF16),
        in_specs=[anywhere] * 5,
        out_specs=pl.BlockSpec(memory_space=pltpu.VMEM),
        scratch_shapes=[
            pltpu.VMEM((2, block, block), BF16),
            pltpu.VMEM((2, block, block), BF16),
            pltpu.VMEM((1, listed), jnp.int32),
            pltpu.VMEM((1, listed), jnp.int32),
            pltpu.SMEM((count,), jnp.int32),
            pltpu.SMEM((count,), jnp.int32),
            pltpu.VMEM((2 * listed, block), BF16),
            pltpu.VMEM((2, 2 * listed, block), BF16),
            pltpu.VMEM((2, 2 * listed, block), BF16),
            pltpu.VMEM((2, 2 * listed, block), BF16),
            pltpu.VMEM((2 * listed, block), F32),
            pltpu.VMEM((count, rows, block), BF16),
            pltpu.VMEM((count, rows, block), BF16),
            pltpu.VMEM((count, rows, block), BF16),
            pltpu.VMEM((count, rows, block), BF16),
            pltpu.VMEM((block // LANES, count * rows, LANES), F32),
            pltpu.SemaphoreType.DMA((5,)),
            pltpu.SemaphoreType.DMA((4,)),
            pltpu.SemaphoreType.DMA((4,)),
            pltpu.SemaphoreType.DMA((count,)),
            pltpu.SemaphoreType.DMA((count,)),
            pltpu.SemaphoreType.DMA((count,)),
            pltpu.SemaphoreType.DMA((count,)),
        ],
        compiler_params=pltpu.CompilerParams(collective_id=0, has_side_effects=True),
    )(green, sigma, tiles, owner, energy_order)
    return result.reshape(1, CAP, 2, count, 1, block)


def solution(mesh):
    placed = (
        P("energy", "slab", None, None, None),
        P("energy", "slab", None, None, None),
        P("slab", None),
        P("slab", None),
        P(),
    )
    return jax.shard_map(
        on_device,
        mesh=mesh,
        in_specs=placed,
        out_specs=P("slab", "energy", None, None, None, None),
        check_vma=False,
    )
```

```python
import functools

import jax
import jax.numpy as jnp
from jax import lax
from jax.experimental import pallas as pl
from jax.experimental.pallas import tpu as pltpu
from jax.sharding import PartitionSpec as P

CAP = 4
LANES = 128
MESH = pl.DeviceIdType.MESH
F32 = jnp.float32
BF16 = jnp.bfloat16


def iota(shape, dim):
    return lax.broadcasted_iota(jnp.int32, shape, dim)


def repeat(first, last, body):
    if last - first <= 16:
        for k in range(first, last):
            body(k)
    else:
        @pl.loop(first, last)
        def _(k):
            body(k)


def column_of(row, length):
    spread = jnp.broadcast_to(row, (length, length))
    eye = iota((length, length), 0) == iota((length, length), 1)
    return jnp.sum(jnp.where(eye, spread, 0.0), axis=1, keepdims=True)


def dot(left, right):
    return jnp.dot(left, right, preferred_element_type=F32)


def dot_t(left, right):
    return lax.dot_general(left, right, (((1,), (1,)), ((), ())), preferred_element_type=F32)


def kernel(
    count,
    slabs,
    green,
    sigma,
    tiles,
    owner,
    order,
    out,
    g_v,
    s_v,
    tiles_v,
    owner_v,
    order_v,
    inverse,
    a_own,
    a_in,
    q_out,
    q_in,
    p_sum,
    d_out,
    d_in,
    l_out,
    l_in,
    lags,
    load_sem,
    slab_send,
    slab_recv,
    d_send,
    d_recv,
    l_send,
    l_recv,
):
    block = g_v.shape[-1]
    listed = tiles_v.shape[-1]
    rows = 2 * CAP
    me = lax.axis_index("energy")
    slab = lax.axis_index("slab")
    parity = lax.rem(slab, 2)
    near = slab + 1 - 2 * parity
    far = slab - 1 + 2 * parity
    has_far = jnp.logical_and(far >= 0, far < slabs)

    loads = [
        pltpu.make_async_copy(tiles, tiles_v, load_sem.at[0]),
        pltpu.make_async_copy(owner, owner_v, load_sem.at[1]),
        pltpu.make_async_copy(order, order_v, load_sem.at[2]),
        pltpu.make_async_copy(green.at[0, 0], g_v, load_sem.at[3]),
        pltpu.make_async_copy(sigma.at[0, 0], s_v, load_sem.at[4]),
    ]
    for load in loads:
        load.start()

    barrier = pltpu.get_barrier_semaphore()

    def greet(k):
        pl.semaphore_signal(
            barrier, inc=1, device_id={"energy": lax.rem(me + k, count)}, device_id_type=MESH
        )

    repeat(1, count, greet)
    pl.semaphore_signal(barrier, inc=1, device_id={"slab": near}, device_id_type=MESH)

    @pl.when(has_far)
    def _():
        pl.semaphore_signal(barrier, inc=1, device_id={"slab": far}, device_id_type=MESH)

    loads[0].wait()
    tile_col = column_of(tiles_v[...].astype(F32), listed)
    onehot = (iota((listed, block), 1).astype(F32) == tile_col).astype(BF16)
    loads[1].wait()
    own_row = owner_v[...].astype(F32)
    own_col = column_of(own_row, listed)
    earlier = (own_col == own_row) & (iota((listed, listed), 1) < iota((listed, listed), 0))
    rank_col = jnp.sum(jnp.where(earlier, 1.0, 0.0), axis=1, keepdims=True)
    slot_col = own_col * CAP + rank_col
    wide = (listed, 2 * listed)
    spread = iota(wide, 0) == lax.rem(iota(wide, 1), listed)
    slot_row = jnp.sum(jnp.where(spread, slot_col, 0.0), axis=0, keepdims=True)
    full = (count * rows, 2 * listed)
    line = iota(full, 0)
    plane = lax.rem(line, rows) // CAP
    slot = (line // rows) * CAP + lax.rem(line, CAP)
    selector = (
        (slot.astype(F32) == slot_row) & (plane == iota(full, 1) // listed)
    ).astype(BF16)

    loads[3].wait()
    row_re = dot(onehot, g_v[0])
    row_im = dot(onehot, g_v[1])
    a_own[0:listed, :] = row_re.astype(BF16)
    a_own[listed : 2 * listed, :] = row_im.astype(BF16)
    d_re = row_re - dot_t(onehot, g_v[0])
    d_im = row_im + dot_t(onehot, g_v[1])
    d_all = jnp.concatenate([d_re, d_im], axis=0).astype(BF16)
    d_out[...] = dot(selector, d_all).astype(BF16).reshape(count, rows, block)

    pl.semaphore_wait(barrier, count + has_far.astype(jnp.int32))

    def to_slab(src, dst, k, target):
        return pltpu.make_async_remote_copy(
            src_ref=src,
            dst_ref=dst,
            send_sem=slab_send.at[k],
            recv_sem=slab_recv.at[k],
            device_id={"slab": target},
            device_id_type=MESH,
        )

    a_far = to_slab(a_own, a_in.at[1], 1, far)
    a_near = to_slab(a_own, a_in.at[0], 0, near)
    q_far = to_slab(q_out.at[1], q_in.at[1], 3, far)
    q_near = to_slab(q_out.at[0], q_in.at[0], 2, near)

    def to_peer(src, dst, send, recv, k):
        peer = lax.rem(me + k, count)
        return pltpu.make_async_remote_copy(
            src_ref=src.at[peer],
            dst_ref=dst.at[me],
            send_sem=send.at[k],
            recv_sem=recv.at[k],
            device_id={"energy": peer},
            device_id_type=MESH,
        )

    @pl.when(has_far)
    def _():
        a_far.start()

    a_near.start()
    repeat(1, count, lambda k: to_peer(d_out, d_in, d_send, d_recv, k).start())
    d_in[me] = d_out[me]

    loads[2].wait()

    def invert(target):
        def step(k, total):
            return jnp.where(order_v[k] == target, k, total)

        inverse[target] = lax.fori_loop(0, count, step, jnp.int32(0), unroll=count <= 16)

    repeat(0, count, invert)

    def times_sigma(a):
        with_re = dot(a, s_v[0])
        with_im = dot(a, s_v[1])
        return (
            with_re[:listed] - with_im[listed:],
            with_im[:listed] + with_re[listed:],
        )

    loads[4].wait()
    own_re, own_im = times_sigma(a_own[...])
    p_sum[0:listed, :] = own_re
    p_sum[listed : 2 * listed, :] = own_im

    def answer(k):
        part_re, part_im = times_sigma(a_in[k])
        q_out[k, 0:listed, :] = part_re.astype(BF16)
        q_out[k, listed : 2 * listed, :] = part_im.astype(BF16)

    a_near.wait_recv()
    answer(0)
    q_near.start()

    @pl.when(has_far)
    def _():
        a_far.wait_recv()
        answer(1)
        q_far.start()

    q_near.wait_recv()
    p_sum[...] += q_in[0].astype(F32)

    @pl.when(has_far)
    def _():
        q_far.wait_recv()
        p_sum[...] += q_in[1].astype(F32)

    p_all = p_sum[...].astype(BF16)
    with_re = dot_t(p_all, g_v[0])
    with_im = dot_t(p_all, g_v[1])
    l_re = with_re[:listed] + with_im[listed:]
    l_im = with_re[listed:] - with_im[:listed]
    l_all = jnp.concatenate([l_re, l_im], axis=0).astype(BF16)
    l_out[...] = dot(selector, l_all).astype(BF16).reshape(count, rows, block)
    repeat(1, count, lambda k: to_peer(l_out, l_in, l_send, l_recv, k).start())
    l_in[me] = l_out[me]

    def arrived(k):
        to_peer(d_out, d_in, d_send, d_recv, k).wait()
        to_peer(l_out, l_in, l_send, l_recv, k).wait()

    repeat(1, count, arrived)

    def lesser_at(point):
        return l_in[inverse[point]].astype(F32)

    def greater_at(point):
        source = inverse[point]
        return l_in[source].astype(F32) + d_in[source].astype(F32)

    upper = iota((rows, block), 0) < CAP

    def finish(straight, crossed):
        return jnp.where(
            upper,
            straight + pltpu.roll(straight, CAP, 0),
            crossed - pltpu.roll(crossed, CAP, 0),
        ) * (1.0 / count)

    def keep(value, where):
        for chunk in range(block // LANES):
            lags[chunk, where, :] = value[:, chunk * LANES : (chunk + 1) * LANES]

    if count <= 8:
        lesser = [lesser_at(e) for e in range(count)]
        greater = [greater_at(e) for e in range(count)]
        swapped = [pltpu.roll(value, CAP, 0) for value in greater]
        for lag in range(count):
            pairs = range(count - lag)
            straight = sum(lesser[e + lag] * greater[e] for e in pairs)
            crossed = sum(lesser[e + lag] * swapped[e] for e in pairs)
            keep(finish(straight, crossed), pl.ds(lag * rows, rows))
    else:
        @pl.loop(0, count)
        def _(lag):
            def step(e, sums):
                left = lesser_at(e + lag)
                right = greater_at(e)
                return (sums[0] + left * right, sums[1] + left * pltpu.roll(right, CAP, 0))

            zero = jnp.zeros((rows, block), F32)
            straight, crossed = lax.fori_loop(0, count - lag, step, (zero, zero))
            keep(finish(straight, crossed), pl.ds(pl.multiple_of(lag * rows, rows), rows))

    for part in range(2):
        for slot_index in range(CAP):
            for chunk in range(block // LANES):
                out[slot_index, part, :, chunk * LANES : (chunk + 1) * LANES] = lags[
                    chunk, pl.ds(part * CAP + slot_index, count, stride=rows), :
                ].astype(BF16)

    a_near.wait_send()
    q_near.wait_send()

    @pl.when(has_far)
    def _():
        a_far.wait_send()
        q_far.wait_send()


def on_device(green, sigma, tiles, owner, energy_order):
    block = green.shape[-1]
    listed = tiles.shape[1]
    count = lax.axis_size("energy")
    slabs = lax.axis_size("slab")
    rows = 2 * CAP
    anywhere = pl.BlockSpec(memory_space=pl.ANY)
    result = pl.pallas_call(
        functools.partial(kernel, count, slabs),
        out_shape=pltpu.VMEM((CAP, 2, count, block), BF16),
        in_specs=[anywhere] * 5,
        out_specs=pl.BlockSpec(memory_space=pltpu.VMEM),
        scratch_shapes=[
            pltpu.VMEM((2, block, block), BF16),
            pltpu.VMEM((2, block, block), BF16),
            pltpu.VMEM((1, listed), jnp.int32),
            pltpu.VMEM((1, listed), jnp.int32),
            pltpu.SMEM((count,), jnp.int32),
            pltpu.SMEM((count,), jnp.int32),
            pltpu.VMEM((2 * listed, block), BF16),
            pltpu.VMEM((2, 2 * listed, block), BF16),
            pltpu.VMEM((2, 2 * listed, block), BF16),
            pltpu.VMEM((2, 2 * listed, block), BF16),
            pltpu.VMEM((2 * listed, block), F32),
            pltpu.VMEM((count, rows, block), BF16),
            pltpu.VMEM((count, rows, block), BF16),
            pltpu.VMEM((count, rows, block), BF16),
            pltpu.VMEM((count, rows, block), BF16),
            pltpu.VMEM((block // LANES, count * rows, LANES), F32),
            pltpu.SemaphoreType.DMA((5,)),
            pltpu.SemaphoreType.DMA((4,)),
            pltpu.SemaphoreType.DMA((4,)),
            pltpu.SemaphoreType.DMA((count,)),
            pltpu.SemaphoreType.DMA((count,)),
            pltpu.SemaphoreType.DMA((count,)),
            pltpu.SemaphoreType.DMA((count,)),
        ],
        compiler_params=pltpu.CompilerParams(collective_id=0, has_side_effects=True),
    )(green, sigma, tiles, owner, energy_order)
    return result.reshape(1, CAP, 2, count, 1, block)


def solution(mesh):
    placed = (
        P("energy", "slab", None, None, None),
        P("energy", "slab", None, None, None),
        P("slab", None),
        P("slab", None),
        P(),
    )
    return jax.shard_map(
        on_device,
        mesh=mesh,
        in_specs=placed,
        out_specs=P("slab", "energy", None, None, None, None),
        check_vma=False,
    )
```

```python
import functools

import jax
import jax.numpy as jnp
from jax import lax
from jax.experimental import pallas as pl
from jax.experimental.pallas import tpu as pltpu
from jax.sharding import PartitionSpec as P

CAP = 4
LANES = 128
MESH = pl.DeviceIdType.MESH
F32 = jnp.float32
BF16 = jnp.bfloat16


def iota(shape, dim):
    return lax.broadcasted_iota(jnp.int32, shape, dim)


def repeat(first, last, body):
    if last - first <= 16:
        for k in range(first, last):
            body(k)
    else:
        @pl.loop(first, last)
        def _(k):
            body(k)


def bits_of(count):
    assert count & (count - 1) == 0 and count > 1
    return [1 << k for k in range(count.bit_length() - 1)]


def column_of(row, length):
    spread = jnp.broadcast_to(row, (length, length))
    eye = iota((length, length), 0) == iota((length, length), 1)
    return jnp.sum(jnp.where(eye, spread, 0.0), axis=1, keepdims=True)


def dot(left, right):
    return jnp.dot(left, right, preferred_element_type=F32)


def dot_t(left, right):
    return lax.dot_general(left, right, (((1,), (1,)), ((), ())), preferred_element_type=F32)


def kernel(
    count,
    slabs,
    green,
    sigma,
    tiles,
    owner,
    order,
    out,
    g_v,
    s_v,
    tiles_v,
    owner_v,
    order_v,
    inverse,
    a_own,
    a_in,
    q_out,
    q_in,
    p_sum,
    d_out,
    d_in,
    l_out,
    l_in,
    lags,
    load_sem,
    slab_send,
    slab_recv,
    d_send,
    d_recv,
    l_send,
    l_recv,
    known,
):
    block = g_v.shape[-1]
    listed = tiles_v.shape[-1]
    rows = 2 * CAP
    me = lax.axis_index("energy")
    slab = lax.axis_index("slab")
    parity = lax.rem(slab, 2)
    near = slab + 1 - 2 * parity
    far = slab - 1 + 2 * parity
    has_far = jnp.logical_and(far >= 0, far < slabs)

    loads = [
        pltpu.make_async_copy(tiles, tiles_v, load_sem.at[0]),
        pltpu.make_async_copy(owner, owner_v, load_sem.at[1]),
        pltpu.make_async_copy(order, order_v, load_sem.at[2]),
        pltpu.make_async_copy(green.at[0, 0], g_v, load_sem.at[3]),
        pltpu.make_async_copy(sigma.at[0, 0], s_v, load_sem.at[4]),
    ]
    for load in loads:
        load.start()

    barrier = pltpu.get_barrier_semaphore()

    partners = [me + bit - 2 * bit * lax.rem(me // bit, 2) for bit in bits_of(count)]
    for partner in partners:
        pl.semaphore_signal(
            barrier, inc=1, device_id={"energy": partner}, device_id_type=MESH
        )
    pl.semaphore_signal(barrier, inc=1, device_id={"slab": near}, device_id_type=MESH)

    @pl.when(has_far)
    def _():
        pl.semaphore_signal(barrier, inc=1, device_id={"slab": far}, device_id_type=MESH)

    loads[0].wait()
    tile_col = column_of(tiles_v[...].astype(F32), listed)
    onehot = (iota((listed, block), 1).astype(F32) == tile_col).astype(BF16)
    loads[1].wait()
    own_row = owner_v[...].astype(F32)
    own_col = column_of(own_row, listed)
    earlier = (own_col == own_row) & (iota((listed, listed), 1) < iota((listed, listed), 0))
    rank_col = jnp.sum(jnp.where(earlier, 1.0, 0.0), axis=1, keepdims=True)
    slot_col = own_col * CAP + rank_col
    wide = (listed, 2 * listed)
    spread = iota(wide, 0) == lax.rem(iota(wide, 1), listed)
    slot_row = jnp.sum(jnp.where(spread, slot_col, 0.0), axis=0, keepdims=True)
    full = (count * rows, 2 * listed)
    line = iota(full, 0)
    plane = lax.rem(line, rows) // CAP
    slot = (line // rows) * CAP + lax.rem(line, CAP)
    selector = (
        (slot.astype(F32) == slot_row) & (plane == iota(full, 1) // listed)
    ).astype(BF16)

    loads[3].wait()
    row_re = dot(onehot, g_v[0])
    row_im = dot(onehot, g_v[1])
    a_own[0:listed, :] = row_re.astype(BF16)
    a_own[listed : 2 * listed, :] = row_im.astype(BF16)
    d_re = row_re - dot_t(onehot, g_v[0])
    d_im = row_im + dot_t(onehot, g_v[1])
    d_all = jnp.concatenate([d_re, d_im], axis=0).astype(BF16)
    d_out[...] = dot(selector, d_all).astype(BF16).reshape(count, rows, block)

    pl.semaphore_wait(barrier, len(partners) + 1 + has_far.astype(jnp.int32))

    def to_slab(src, dst, k, target):
        return pltpu.make_async_remote_copy(
            src_ref=src,
            dst_ref=dst,
            send_sem=slab_send.at[k],
            recv_sem=slab_recv.at[k],
            device_id={"slab": target},
            device_id_type=MESH,
        )

    a_far = to_slab(a_own, a_in.at[1], 1, far)
    a_near = to_slab(a_own, a_in.at[0], 0, near)
    q_far = to_slab(q_out.at[1], q_in.at[1], 3, far)
    q_near = to_slab(q_out.at[0], q_in.at[0], 2, near)

    def to_peer(src, dst, send, recv, k):
        peer = lax.rem(me + k, count)
        return pltpu.make_async_remote_copy(
            src_ref=src.at[peer],
            dst_ref=dst.at[me],
            send_sem=send.at[k],
            recv_sem=recv.at[k],
            device_id={"energy": peer},
            device_id_type=MESH,
        )

    @pl.when(has_far)
    def _():
        a_far.start()

    a_near.start()
    d_in[me] = d_out[me]

    rounds = len(partners) - 1

    def tell(k):
        if k < rounds:
            pl.semaphore_signal(
                known.at[k], inc=1, device_id={"energy": partners[k]}, device_id_type=MESH
            )

    def hear(k):
        if k < rounds:
            pl.semaphore_wait(known.at[k], 1)

    tell(0)

    loads[2].wait()

    def invert(target):
        def step(k, total):
            return jnp.where(order_v[k] == target, k, total)

        inverse[target] = lax.fori_loop(0, count, step, jnp.int32(0), unroll=count <= 16)

    repeat(0, count, invert)

    def times_sigma(a):
        with_re = dot(a, s_v[0])
        with_im = dot(a, s_v[1])
        return (
            with_re[:listed] - with_im[listed:],
            with_im[:listed] + with_re[listed:],
        )

    loads[4].wait()
    own_re, own_im = times_sigma(a_own[...])
    p_sum[0:listed, :] = own_re
    p_sum[listed : 2 * listed, :] = own_im
    hear(0)
    tell(1)

    def answer(k):
        part_re, part_im = times_sigma(a_in[k])
        q_out[k, 0:listed, :] = part_re.astype(BF16)
        q_out[k, listed : 2 * listed, :] = part_im.astype(BF16)

    a_near.wait_recv()
    answer(0)
    q_near.start()

    @pl.when(has_far)
    def _():
        a_far.wait_recv()
        answer(1)
        q_far.start()

    hear(1)
    for k in range(2, rounds):
        tell(k)
        hear(k)
    repeat(1, count, lambda k: to_peer(d_out, d_in, d_send, d_recv, k).start())

    q_near.wait_recv()
    p_sum[...] += q_in[0].astype(F32)

    @pl.when(has_far)
    def _():
        q_far.wait_recv()
        p_sum[...] += q_in[1].astype(F32)

    p_all = p_sum[...].astype(BF16)
    with_re = dot_t(p_all, g_v[0])
    with_im = dot_t(p_all, g_v[1])
    l_re = with_re[:listed] + with_im[listed:]
    l_im = with_re[listed:] - with_im[:listed]
    l_all = jnp.concatenate([l_re, l_im], axis=0).astype(BF16)
    l_out[...] = dot(selector, l_all).astype(BF16).reshape(count, rows, block)
    repeat(1, count, lambda k: to_peer(l_out, l_in, l_send, l_recv, k).start())
    l_in[me] = l_out[me]

    def arrived(k):
        to_peer(d_out, d_in, d_send, d_recv, k).wait()
        to_peer(l_out, l_in, l_send, l_recv, k).wait()

    repeat(1, count, arrived)

    def lesser_at(point):
        return l_in[inverse[point]].astype(F32)

    def greater_at(point):
        source = inverse[point]
        return l_in[source].astype(F32) + d_in[source].astype(F32)

    upper = iota((rows, block), 0) < CAP

    def finish(straight, crossed):
        return jnp.where(
            upper,
            straight + pltpu.roll(straight, CAP, 0),
            crossed - pltpu.roll(crossed, CAP, 0),
        ) * (1.0 / count)

    def keep(value, where):
        for chunk in range(block // LANES):
            lags[chunk, where, :] = value[:, chunk * LANES : (chunk + 1) * LANES]

    if count <= 8:
        lesser = [lesser_at(e) for e in range(count)]
        greater = [greater_at(e) for e in range(count)]
        swapped = [pltpu.roll(value, CAP, 0) for value in greater]
        for lag in range(count):
            pairs = range(count - lag)
            straight = sum(lesser[e + lag] * greater[e] for e in pairs)
            crossed = sum(lesser[e + lag] * swapped[e] for e in pairs)
            keep(finish(straight, crossed), pl.ds(lag * rows, rows))
    else:
        @pl.loop(0, count)
        def _(lag):
            def step(e, sums):
                left = lesser_at(e + lag)
                right = greater_at(e)
                return (sums[0] + left * right, sums[1] + left * pltpu.roll(right, CAP, 0))

            zero = jnp.zeros((rows, block), F32)
            straight, crossed = lax.fori_loop(0, count - lag, step, (zero, zero))
            keep(finish(straight, crossed), pl.ds(pl.multiple_of(lag * rows, rows), rows))

    for part in range(2):
        for slot_index in range(CAP):
            for chunk in range(block // LANES):
                out[slot_index, part, :, chunk * LANES : (chunk + 1) * LANES] = lags[
                    chunk, pl.ds(part * CAP + slot_index, count, stride=rows), :
                ].astype(BF16)

    a_near.wait_send()
    q_near.wait_send()

    @pl.when(has_far)
    def _():
        a_far.wait_send()
        q_far.wait_send()


def on_device(green, sigma, tiles, owner, energy_order):
    block = green.shape[-1]
    listed = tiles.shape[1]
    count = lax.axis_size("energy")
    slabs = lax.axis_size("slab")
    rows = 2 * CAP
    anywhere = pl.BlockSpec(memory_space=pl.ANY)
    result = pl.pallas_call(
        functools.partial(kernel, count, slabs),
        out_shape=pltpu.VMEM((CAP, 2, count, block), BF16),
        in_specs=[anywhere] * 5,
        out_specs=pl.BlockSpec(memory_space=pltpu.VMEM),
        scratch_shapes=[
            pltpu.VMEM((2, block, block), BF16),
            pltpu.VMEM((2, block, block), BF16),
            pltpu.VMEM((1, listed), jnp.int32),
            pltpu.VMEM((1, listed), jnp.int32),
            pltpu.SMEM((count,), jnp.int32),
            pltpu.SMEM((count,), jnp.int32),
            pltpu.VMEM((2 * listed, block), BF16),
            pltpu.VMEM((2, 2 * listed, block), BF16),
            pltpu.VMEM((2, 2 * listed, block), BF16),
            pltpu.VMEM((2, 2 * listed, block), BF16),
            pltpu.VMEM((2 * listed, block), F32),
            pltpu.VMEM((count, rows, block), BF16),
            pltpu.VMEM((count, rows, block), BF16),
            pltpu.VMEM((count, rows, block), BF16),
            pltpu.VMEM((count, rows, block), BF16),
            pltpu.VMEM((block // LANES, count * rows, LANES), F32),
            pltpu.SemaphoreType.DMA((5,)),
            pltpu.SemaphoreType.DMA((4,)),
            pltpu.SemaphoreType.DMA((4,)),
            pltpu.SemaphoreType.DMA((count,)),
            pltpu.SemaphoreType.DMA((count,)),
            pltpu.SemaphoreType.DMA((count,)),
            pltpu.SemaphoreType.DMA((count,)),
            pltpu.SemaphoreType.REGULAR((len(bits_of(count)),)),
        ],
        compiler_params=pltpu.CompilerParams(collective_id=0, has_side_effects=True),
    )(green, sigma, tiles, owner, energy_order)
    return result.reshape(1, CAP, 2, count, 1, block)


def solution(mesh):
    placed = (
        P("energy", "slab", None, None, None),
        P("energy", "slab", None, None, None),
        P("slab", None),
        P("slab", None),
        P(),
    )
    return jax.shard_map(
        on_device,
        mesh=mesh,
        in_specs=placed,
        out_specs=P("slab", "energy", None, None, None, None),
        check_vma=False,
    )
```
